128 devices in a mesh: gr: 16 (over x, y_hi, core), gc: 8 (over z, y_lo).
Axes of the slice: x: 4, y: 4 (y_hi: 2, y_lo: 2; y = y_hi * 2 + y_lo), z: 4, core: 2. Of those that a mesh axis runs over, the one named last changes fastest.
Arguments:
- returns: bfloat16 [16384, 8192], P(('gr', 'gc')), may hold values from -6 to 6
- start_seed: int32 [8192, 64], replicated, may hold values from -1000 to 999
Outputs:
- loadings: float32 [8192, 64], P('gr')
- strengths: float32 [3, 64], replicated
The draws below stay inside these ranges and needn't reach their ends.
All inputs are finite; a program needn't handle non-finite values.
Results may differ from the reference program's by a relative error of at most 0.0003.
Values may be sent and summed in bfloat16 or wider, within the bound.
A program may use at most 128 MiB of HBM per device.

```python
import math
import jax
import jax.numpy as jnp
from jax import lax

ASSETS = 8192
FACTORS = 64
ITERS = 3
DAYS = 16384


def with_ends(entries, own_key, low, high):
    index_at = [jax.random.randint(jax.random.fold_in(own_key, axis), (), 0, length) for axis, length in enumerate(entries.shape)]
    longest = entries.shape.index(max(entries.shape))
    next_to = index_at[:longest] + [(index_at[longest] + 1) % entries.shape[longest]] + index_at[longest + 1:]
    return entries.at[tuple(index_at)].set(low).at[tuple(next_to)].set(high)


def levels(key, shape, cuts, least, top_value):
    def one(dim, parts):
        steps = jax.random.uniform(jax.random.fold_in(jax.random.fold_in(key, 6), dim), (parts,), jnp.float32, least / len(cuts), top_value / len(cuts))
        return jnp.repeat(jnp.exp(steps), shape[dim] // parts).reshape((-1,) + (1,) * (len(shape) - dim - 1))

    gain = one(*cuts[0])
    for cut in cuts[1:]:
        gain = gain * one(*cut)
    return gain


def normal_values(rng, dims, deviation, bound, cuts=(), dtype=jnp.bfloat16):
    entries = deviation * jax.random.normal(rng, dims, jnp.float32)
    if cuts:
        entries = entries * levels(rng, dims, cuts, -0.22, 0.18)
    return jnp.clip(entries, -bound, bound).astype(dtype)


def setup_inputs(seed: int = 0) -> dict:
    key_of = jax.random.split(jax.random.key(seed), 3)
    returns = normal_values(key_of[0], (DAYS, ASSETS), 1.0, 6.0, ((0, 128),))
    start_seed = with_ends(jax.random.randint(key_of[1], (ASSETS, FACTORS), -1000, 1000), jax.random.fold_in(key_of[1], 1), -1000, 999).astype(jnp.int32)
    return dict(returns=returns, start_seed=start_seed)


def orthonormal(applied):
    inner_gram = jnp.dot(applied.T, applied, precision=lax.Precision.HIGHEST)
    factor = jnp.linalg.cholesky(inner_gram)
    solved = lax.linalg.triangular_solve(factor, applied, left_side=False, lower=True, transpose_a=True)
    return (solved, jnp.diagonal(factor))

def reference(returns, start_seed):
    covariance = jnp.dot(returns.T.astype(jnp.float32), returns.astype(jnp.float32), preferred_element_type=jnp.float32) / DAYS
    vectors = start_seed.astype(jnp.float32) / 1000.0
    diagonals = []
    for sweep in range(ITERS):
        applied = jnp.dot(covariance, vectors, precision=lax.Precision.HIGHEST)
        vectors, diag_part = orthonormal(applied)
        diagonals.append(diag_part)
    return (vectors * math.sqrt(ASSETS), jnp.stack(diagonals, axis=0))
```

```python
import functools
import math

import jax
import jax.numpy as jnp
from jax import lax
from jax.experimental import pallas as pl
from jax.experimental.pallas import tpu as pltpu
from jax.sharding import PartitionSpec as P

ITERS = 3
MESH = pl.DeviceIdType.MESH
F32 = jnp.float32
BF16 = jnp.bfloat16
NT = (((1,), (1,)), ((), ()))


def split3(a):
    hi = a.astype(BF16)
    rest = a - hi.astype(F32)
    mid = rest.astype(BF16)
    low = (rest - mid.astype(F32)).astype(BF16)
    return jnp.concatenate([hi, mid, low], axis=0)


def fold3(a):
    return a[0:64] + (a[64:128] + a[128:192])


def factor(gram):
    lane = lax.broadcasted_iota(jnp.int32, (8, 128), 1)
    sub = lax.broadcasted_iota(jnp.int32, (8, 128), 0)
    wide = jnp.concatenate([jnp.zeros((64, 64), F32), gram], axis=1)
    rows = [
        jnp.where(lane == sub + 8 * g, 1.0, wide[8 * g : 8 * g + 8]) for g in range(8)
    ]
    for j in range(64):
        g0, r = divmod(j, 8)
        pivot = jnp.broadcast_to(rows[g0][r : r + 1, :], (8, 128))
        d = jnp.broadcast_to(pivot[:, 64 + j : 65 + j], (8, 128))
        scaled = pivot / d
        for g in range(g0, 8):
            col = jnp.broadcast_to(rows[g][:, 64 + j : 65 + j], (8, 128))
            if g == g0:
                col = jnp.where(sub > r, col, 0.0)
            rows[g] = rows[g] - col * scaled
    inverse = []
    diag = jnp.zeros((8, 128), F32)
    for g in range(8):
        mask = lane == sub + (8 * g + 64)
        d = jnp.sum(jnp.where(mask, rows[g], 0.0), axis=1, keepdims=True)
        root = jnp.broadcast_to(jnp.sqrt(d), (8, 128))
        inverse.append(rows[g] / root)
        diag = diag + jnp.where(mask, root, 0.0)
    inverse = jnp.concatenate(inverse, axis=0)[:, 0:64]
    return inverse, jnp.sum(diag, axis=0, keepdims=True)[:, 64:128]


def kernel(
    days, r_ref, seed_ref, load_ref, str_ref,
    rb, seeds, pbuf, pc, abuf, r1, bbuf, r2, ybuf, ag, gbuf, fin, gx, gz,
    send, recv,
):
    gr = lax.axis_index("gr")
    gc = lax.axis_index("gc")
    core = gr % 2
    x = gr // 4
    y = (gr // 2) % 2 * 2 + gc % 2
    z = gc // 2

    def dev(x, y, z, core):
        return ((x * 2 + y // 2) * 2 + core, z * 2 + y % 2)

    partner = dev(x, y, z, 1 - core)
    xp = [dev((x + o) % 4, y, z, core) for o in (1, 2, 3)]
    yp = [dev(x, (y + o) % 4, z, core) for o in (1, 2, 3)]
    zp = [dev(x, y, (z + o) % 4, core) for o in (1, 2, 3)]

    barrier = pltpu.get_barrier_semaphore()
    everyone = [partner] + xp + yp + zp
    for device in everyone:
        pl.semaphore_signal(barrier, inc=1, device_id=device, device_id_type=MESH)
    pl.semaphore_wait(barrier, len(everyone))

    count = [0]
    pending = []

    def push(src, dst, device):
        k = count[0]
        count[0] += 1
        copy = pltpu.make_async_remote_copy(
            src_ref=src, dst_ref=dst, send_sem=send.at[k], recv_sem=recv.at[k],
            device_id=device, device_id_type=MESH,
        )
        copy.start()
        pending.append(copy)
        return copy

    mine = pl.ds(pl.multiple_of(core * 128, 128), 128)
    swaps = []
    for s in range(8):
        cols = pl.ds(pl.multiple_of((2 * s + 1 - core) * 512, 512), 512)
        swaps.append(push(r_ref.at[:, cols], rb.at[mine, pl.ds(s * 512, 512)], partner))
    for s in range(8):
        cols = pl.ds(pl.multiple_of((2 * s + core) * 512, 512), 512)
        rb[mine, pl.ds(s * 512, 512)] = r_ref[:, cols]

    for c in range(8):
        part = seed_ref[:, c * 1024 : (c + 1) * 1024].astype(F32)
        hi = part.astype(BF16)
        low = (part - hi.astype(F32)).astype(BF16)
        seeds[0:64, c * 1024 : (c + 1) * 1024] = hi
        seeds[64:128, c * 1024 : (c + 1) * 1024] = low
    first = lax.dot_general(seeds[...], r_ref[...], NT, preferred_element_type=F32)
    pbuf[0, core, :, 0:128] = (first[0:64] + first[64:128]) / 1000.0
    copy = push(pbuf.at[0, core, :, 0:128], pbuf.at[0, core, :, 0:128], partner)
    copy.wait_recv()
    for swap in swaps:
        swap.wait_recv()
    projected = jnp.concatenate([pbuf[0, 0, :, 0:128], pbuf[0, 1, :, 0:128]], axis=1)

    peers = ((xp, zp), (zp, xp))
    place = ((x, z), (z, x))
    inverse = None
    for it in range(ITERS):
        p3 = split3(projected * (1.0 / days))
        for s in range(8):
            out = fold3(jnp.dot(p3, rb[:, s * 512 : (s + 1) * 512], preferred_element_type=F32))
            for j in range(4):
                h, xq = s % 2, s // 2
                block = out[:, j * 128 : (j + 1) * 128]
                if h == 0:
                    abuf[it, 0, xq, j] = block
                else:
                    abuf[it, 1, j, xq] = block
        copies = []
        for h in range(2):
            for o in (1, 0, 2):
                to = (place[h][0] + o + 1) % 4
                copies.append(push(abuf.at[it, h, to], r1.at[it, h, o], peers[h][0][o]))
        if it > 0:
            square = fold_gram(lax.dot_general(pc[...], pc[...], NT, preferred_element_type=F32))
            gbuf[it - 1, core, :, 0:64] = square
            copy = push(gbuf.at[it - 1, core], gbuf.at[it - 1, core], partner)
            copy.wait_recv()
            inverse, diag = factor(gbuf[it - 1, 0, :, 0:64] + gbuf[it - 1, 1, :, 0:64])
            str_ref[it - 1 : it, :] = diag
        for copy in copies:
            copy.wait_recv()
        copies = []
        for h in range(2):
            bbuf[it, h] = (abuf[it, h, place[h][0]] + r1[it, h, 0]) + (r1[it, h, 1] + r1[it, h, 2])
        for h in range(2):
            for o in (1, 0, 2):
                to = (place[h][1] + o + 1) % 4
                copies.append(push(bbuf.at[it, h, to], r2.at[it, h, o], peers[h][1][o]))
        for copy in copies:
            copy.wait_recv()
        for h in range(2):
            ybuf[it, y, h] = (bbuf[it, h, place[h][1]] + r2[it, h, 0]) + (r2[it, h, 1] + r2[it, h, 2])
        copies = [push(ybuf.at[it, y], ybuf.at[it, y], yp[o]) for o in (1, 0, 2)]
        for copy in copies:
            copy.wait_recv()
        done = [(ybuf[it, 0, h] + ybuf[it, 1, h]) + (ybuf[it, 2, h] + ybuf[it, 3, h]) for h in range(2)]
        if it > 0:
            both = jnp.dot(inverse, jnp.concatenate(done, axis=1), precision=lax.Precision.HIGHEST, preferred_element_type=F32)
            done = [both[:, 0:128], both[:, 128:256]]
        if it == ITERS - 1:
            break
        copies = []
        for h in range(2):
            ag[it, h, place[h][0], place[h][1]] = done[h]
        for h in range(2):
            block = ag.at[it, h, place[h][0], place[h][1]]
            for o in (1, 0, 2):
                copies.append(push(block, block, peers[h][1][o]))
        for copy in copies:
            copy.wait_recv()
        copies = []
        for h in range(2):
            block = ag.at[it, h, place[h][0]]
            for o in (1, 0, 2):
                copies.append(push(block, block, peers[h][0][o]))
        for copy in copies:
            copy.wait_recv()
        for s in range(8):
            for j in range(4):
                h, xq = s % 2, s // 2
                block = ag[it, 0, xq, j] if h == 0 else ag[it, 1, j, xq]
                pc[:, (4 * s + j) * 128 : (4 * s + j + 1) * 128] = split3(block)
        pbuf[it + 1, core] = fold3(lax.dot_general(pc[...], rb[...], NT, preferred_element_type=F32))
        copy = push(pbuf.at[it + 1, core], pbuf.at[it + 1, core], partner)
        copy.wait_recv()
        projected = pbuf[it + 1, 0] + pbuf[it + 1, 1]

    fin[z] = jnp.where(y < 2, done[0], done[1])
    last = [push(fin.at[z], fin.at[z], zp[o]) for o in (1, 0, 2)]
    whole = jnp.concatenate(done, axis=1)
    wide = split3(whole)
    gx[x, :, 0:64] = fold_gram(lax.dot_general(wide, wide, NT, preferred_element_type=F32))
    copies = [push(gx.at[x], gx.at[x], xp[o]) for o in (1, 0, 2)]
    for copy in copies:
        copy.wait_recv()
    gz[z] = (gx[0] + gx[1]) + (gx[2] + gx[3])
    copies = [push(gz.at[z], gz.at[z], zp[o]) for o in (1, 0, 2)]
    for copy in copies:
        copy.wait_recv()
    gbuf[2, core] = (gz[0] + gz[1]) + (gz[2] + gz[3])
    copy = push(gbuf.at[2, core], gbuf.at[2, core], partner)
    copy.wait_recv()
    inverse, diag = factor(gbuf[2, 0, :, 0:64] + gbuf[2, 1, :, 0:64])
    str_ref[2:3, :] = diag
    for copy in last:
        copy.wait_recv()
    slab = jnp.concatenate([fin[k] for k in range(4)], axis=1)
    out = jnp.dot(inverse, slab, precision=lax.Precision.HIGHEST, preferred_element_type=F32)
    load_ref[...] = out * math.sqrt(8192)
    for copy in pending:
        copy.wait_send()


def fold_gram(a):
    hh, hm, hl = a[0:64, 0:64], a[0:64, 64:128], a[0:64, 128:192]
    mh, mm, lh = a[64:128, 0:64], a[64:128, 64:128], a[128:192, 0:64]
    return hh + ((hm + mh) + (mm + (hl + lh)))


SEMS = 128


def local(days, returns, start_seed):
    seed = start_seed.T
    vm = pltpu.VMEM
    out = pl.pallas_call(
        functools.partial(kernel, days),
        out_shape=(
            jax.ShapeDtypeStruct((64, 512), F32),
            jax.ShapeDtypeStruct((3, 64), F32),
        ),
        in_specs=[pl.BlockSpec(memory_space=pltpu.VMEM)] * 2,
        out_specs=[pl.BlockSpec(memory_space=pltpu.VMEM)] * 2,
        scratch_shapes=[
            vm((256, 4096), BF16),
            vm((128, 8192), BF16),
            vm((3, 2, 64, 256), F32),
            vm((192, 4096), BF16),
            vm((3, 2, 4, 4, 64, 128), F32),
            vm((3, 2, 3, 4, 64, 128), F32),
            vm((3, 2, 4, 64, 128), F32),
            vm((3, 2, 3, 64, 128), F32),
            vm((3, 4, 2, 64, 128), F32),
            vm((2, 2, 4, 4, 64, 128), F32),
            vm((3, 2, 64, 128), F32),
            vm((4, 64, 128), F32),
            vm((4, 64, 128), F32),
            vm((4, 64, 128), F32),
            pltpu.SemaphoreType.DMA((SEMS,)),
            pltpu.SemaphoreType.DMA((SEMS,)),
        ],
        compiler_params=pltpu.CompilerParams(
            collective_id=0, has_side_effects=True, vmem_limit_bytes=40 * 2**20
        ),
        name="power",
    )(returns, seed)
    return out[0].T, out[1]


def solution(mesh):
    placed = (P(("gr", "gc"), None), P())
    return jax.shard_map(
        functools.partial(local, 16384), mesh=mesh, in_specs=placed,
        out_specs=(P("gr", None), P()), check_vma=False,
    )
```

```python
import functools
import math

import jax
import jax.numpy as jnp
from jax import lax
from jax.experimental import pallas as pl
from jax.experimental.pallas import tpu as pltpu
from jax.sharding import PartitionSpec as P

ITERS = 3
MESH = pl.DeviceIdType.MESH
F32 = jnp.float32
BF16 = jnp.bfloat16
NN = (((1,), (0,)), ((), ()))
NT = (((1,), (1,)), ((), ()))


def dot(a, b, dims=NN):
    return lax.dot_general(a, b, dims, preferred_element_type=F32)


def exact(a, b, dims=NN):
    return lax.dot_general(a, b, dims, precision=lax.Precision.HIGHEST, preferred_element_type=F32)


def split3(a):
    hi = a.astype(BF16)
    rest = a - hi.astype(F32)
    mid = rest.astype(BF16)
    low = (rest - mid.astype(F32)).astype(BF16)
    return jnp.concatenate([hi, mid, low], axis=0)


def fold(a):
    return a[0:32] + (a[32:64] + a[64:96])


def fold2(a):
    hh, hm, hl = a[0:32, 0:32], a[0:32, 32:64], a[0:32, 64:96]
    mh, mm, lh = a[32:64, 0:32], a[32:64, 32:64], a[64:96, 0:32]
    return hh + ((hm + mh) + (mm + (hl + lh)))


def factor32(gram):
    lane = lax.broadcasted_iota(jnp.int32, (8, 128), 1)
    sub = lax.broadcasted_iota(jnp.int32, (8, 128), 0)
    bc = lambda a: jnp.broadcast_to(a, (8, 128))
    zero = jnp.zeros((32, 32), F32)
    wide = jnp.concatenate([zero, zero, gram, zero], axis=1)
    rows = [jnp.where(lane == sub + 8 * g, 1.0, wide[8 * g : 8 * g + 8]) for g in range(4)]
    for j in range(0, 32, 4):
        g0, r = divmod(j, 8)
        cols = [[bc(rows[g][:, 64 + j + k : 65 + j + k]) for g in range(g0, 4)] for k in range(4)]
        p = [bc(rows[g0][r + k : r + k + 1, :]) for k in range(4)]
        a = [[bc(cols[k][0][r + i : r + i + 1, :]) for k in range(i + 1)] for i in range(4)]
        idet = 1.0 / (a[0][0] * a[1][1] - a[1][0] * a[1][0])
        s = (a[1][1] * p[0] - a[1][0] * p[1]) * idet
        t = (a[0][0] * p[1] - a[1][0] * p[0]) * idet
        s2 = (a[1][1] * a[2][0] - a[1][0] * a[2][1]) * idet
        t2 = (a[0][0] * a[2][1] - a[1][0] * a[2][0]) * idet
        s3 = (a[1][1] * a[3][0] - a[1][0] * a[3][1]) * idet
        t3 = (a[0][0] * a[3][1] - a[1][0] * a[3][0]) * idet
        a22 = a[2][2] - (a[2][0] * s2 + a[2][1] * t2)
        a32 = a[3][2] - (a[3][0] * s2 + a[3][1] * t2)
        a33 = a[3][3] - (a[3][0] * s3 + a[3][1] * t3)
        p2 = p[2] - (a[2][0] * s + a[2][1] * t)
        p3 = p[3] - (a[3][0] * s + a[3][1] * t)
        idet = 1.0 / (a22 * a33 - a32 * a32)
        u = (a33 * p2 - a32 * p3) * idet
        v = (a22 * p3 - a32 * p2) * idet
        s = s - (s2 * u + s3 * v)
        t = t - (t2 * u + t3 * v)
        for g in range(g0, 4):
            c = [cols[k][g - g0] for k in range(4)]
            new = rows[g] - ((c[0] * s + c[1] * t) + (c[2] * u + c[3] * v))
            if g == g0:
                p1 = p[1] - a[1][0] / a[0][0] * p[0]
                p3 = p3 - a32 / a22 * p2
                new = jnp.where(sub < r + 4, rows[g], new)
                new = jnp.where(sub == r + 1, p1, new)
                new = jnp.where(sub == r + 2, p2, new)
                new = jnp.where(sub == r + 3, p3, new)
            rows[g] = new
    inverse = []
    diag = jnp.zeros((8, 128), F32)
    for g in range(4):
        mask = lane == sub + (8 * g + 64)
        d = jnp.sum(jnp.where(mask, rows[g], 0.0), axis=1, keepdims=True)
        root = bc(jnp.sqrt(d))
        inverse.append(rows[g] / root)
        diag = diag + jnp.where(mask, root, 0.0)
    return jnp.concatenate(inverse, axis=0)[:, 0:32], jnp.sum(diag, axis=0, keepdims=True)[:, 64:96]


def kernel(
    days, r_ref, seed_ref, load_ref, str_ref,
    rb, rv, sv, pbuf, pc, abuf, r1, bbuf, r2, ybuf, ag, gbuf, fin, ga,
    local, send, recv,
):
    gr = lax.axis_index("gr")
    gc = lax.axis_index("gc")
    core = gr % 2
    x = gr // 4
    y = (gr // 2) % 2 * 2 + gc % 2
    z = gc // 2

    def dev(x, y, z, core):
        return ((x * 2 + y // 2) * 2 + core, z * 2 + y % 2)

    partner = dev(x, y, z, 1 - core)
    order = (1, 0, 2)
    xp = [dev((x + o) % 4, y, z, core) for o in (1, 2, 3)]
    yp = [dev(x, (y + o) % 4, z, core) for o in (1, 2, 3)]
    zp = [dev(x, y, (z + o) % 4, core) for o in (1, 2, 3)]
    plane = [dev((x + k // 4) % 4, y, (z + k % 4) % 4, core) for k in range(1, 16)]

    barrier = pltpu.get_barrier_semaphore()
    everyone = [partner] + xp + yp + zp
    for device in everyone:
        pl.semaphore_signal(barrier, inc=1, device_id=device, device_id_type=MESH)

    mine = pl.ds(pl.multiple_of(core * 128, 128), 128)
    loads = []
    for s in range(8):
        here = pl.ds(s * 1024, 1024)
        loads.append(
            (
                pltpu.make_async_copy(seed_ref.at[:, here], sv.at[:, here], local.at[s]),
                pltpu.make_async_copy(r_ref.at[:, here], rv.at[:, here], local.at[8 + s]),
            )
        )
        for copy in loads[s]:
            copy.start()
    spots = [(2 * q, 0, 512, q * 512) for q in range(4)]
    spots += [(2 * q + 1, j * 128, 128, 2048 + j * 512 + q * 128) for q in range(4) for j in range(4)]

    def columns(slab, offset, width, side):
        return r_ref.at[:, pl.ds(pl.multiple_of((slab * 2 + side) * 512 + offset, 128), width)]

    for slab, offset, width, spot in spots:
        here = rb.at[mine, pl.ds(spot, width)]
        pltpu.make_async_copy(columns(slab, offset, width, core), here, local.at[16]).start()
    halves = pltpu.make_async_copy(r_ref.at[:, 0:4096], rb.at[mine], local.at[16])

    pl.semaphore_wait(barrier, len(everyone))

    count = [0]
    pending = []

    def group(region, parts):
        k = count[0]
        count[0] += 1
        for src, dst, device in parts:
            pltpu.make_async_remote_copy(
                src_ref=src, dst_ref=dst, send_sem=send.at[k], recv_sem=recv.at[k],
                device_id=device, device_id_type=MESH,
            ).start()
        whole = pltpu.make_async_remote_copy(
            src_ref=region, dst_ref=region, send_sem=send.at[k], recv_sem=recv.at[k],
            device_id=partner, device_id_type=MESH,
        )
        pending.append(whole)
        return whole

    def single(ref, device):
        return group(ref, [(ref, ref, device)])

    swaps = group(
        rb.at[0:128],
        [
            (columns(slab, offset, width, 1 - core), rb.at[mine, pl.ds(spot, width)], partner)
            for slab, offset, width, spot in spots
        ],
    )

    rows = [slice(32 * c, 32 * c + 32) for c in range(2)]
    pieces = [slice(96 * c, 96 * c + 96) for c in range(2)]
    peers = ((xp, zp), (zp, xp))
    place = ((x, z), (z, x))
    swap_p = [None, None]

    first = None
    for s in range(8):
        here = slice(s * 1024, (s + 1) * 1024)
        for copy in loads[s]:
            copy.wait()
        part = sv[:, here].astype(F32)
        hi = part.astype(BF16)
        part = jnp.concatenate([hi, (part - hi.astype(F32)).astype(BF16)], axis=0)
        part = dot(part, rv[:, here], NT)
        first = part if first is None else first + part
    first = (first[0:64] + first[64:128]) / 1000.0
    pbuf[0, core, :, 0:128] = first
    swap_p[0] = single(pbuf.at[0, core, :, 0:128], partner)
    halves.wait()
    swap_p[0].wait_recv()
    first = jnp.concatenate([pbuf[0, 0, :, 0:128], pbuf[0, 1, :, 0:128]], axis=1)
    swaps.wait_recv()

    def part(h, p):
        return pl.ds(pl.multiple_of(h * 2048 + p * 512, 512), 512)

    def product(it, c):
        if it > 0:
            swap_p[c].wait_recv()
            p3 = split3((pbuf[it, 0, rows[c]] + pbuf[it, 1, rows[c]]) * (1.0 / days))
        else:
            p3 = split3(first[rows[c]] * (1.0 / days))
        moving = []
        for o in order + (3,):
            for h in range(2):
                to = (place[h][0] + o + 1) % 4
                out = fold(dot(p3, rb[:, part(h, to)]))
                for j in range(4):
                    abuf[it, c, h, to, j] = out[:, j * 128 : (j + 1) * 128]
            if o < 3:
                parts = []
                for h in range(2):
                    to = (place[h][0] + o + 1) % 4
                    parts.append((abuf.at[it, c, h, to], r1.at[it, c, h, o], peers[h][0][o]))
                moving.append(group(r1.at[it, c, 0, 0:2], parts))
        return moving

    def second(it, c, moving):
        for copy in moving:
            copy.wait_recv()
        parts = []
        for h in range(2):
            bbuf[it, c, h] = (abuf[it, c, h, place[h][0]] + r1[it, c, h, 0]) + (r1[it, c, h, 1] + r1[it, c, h, 2])
            for o in order:
                to = (place[h][1] + o + 1) % 4
                parts.append((bbuf.at[it, c, h, to], r2.at[it, c, h, o], peers[h][1][o]))
        return group(r2.at[it, c], parts)

    def third(it, c, moving):
        moving.wait_recv()
        for h in range(2):
            ybuf[it, c, y, h] = (bbuf[it, c, h, place[h][1]] + r2[it, c, h, 0]) + (r2[it, c, h, 1] + r2[it, c, h, 2])
        here = ybuf.at[it, c, y]
        return group(ybuf.at[it, c, 0:3], [(here, here, yp[o]) for o in order])

    def reduced(it, c, moving):
        moving.wait_recv()
        return jnp.concatenate(
            [(ybuf[it, c, 0, h] + ybuf[it, c, 1, h]) + (ybuf[it, c, 2, h] + ybuf[it, c, 3, h]) for h in range(2)],
            axis=1,
        )

    def gather1(it, c, done):
        parts = []
        for h in range(2):
            ag[it, c, h, place[h][0], place[h][1]] = done[:, 128 * h : 128 * h + 128]
        for h in range(2):
            block = ag.at[it, c, h, place[h][0], place[h][1]]
            parts += [(block, block, peers[h][1][o]) for o in order]
        return group(r2.at[it, c], parts)

    def gather2(it, c, moving):
        moving.wait_recv()
        sent = []
        for o in order:
            parts = []
            for h in range(2):
                block = ag.at[it, c, h, place[h][0]]
                parts.append((block, block, peers[h][0][o]))
            sent.append(group(r1.at[it, c, 0, 0:2], parts))
        return sent, project(it, c, 3)

    def project(it, c, o):
        total = None
        for h in range(2):
            p = (place[h][0] + 3 - o) % 4
            piece = split3(jnp.concatenate([ag[it, c, h, p, j] for j in range(4)], axis=1))
            pc[pieces[c], part(h, p)] = piece
            term = dot(piece, rb[:, part(h, p)], NT)
            total = term if total is None else total + term
        return total

    def projected(it, c, sent, total):
        for o, copy in zip(order, sent):
            copy.wait_recv()
            total = total + project(it, c, o)
        pbuf[it + 1, core, rows[c]] = fold(total)
        swap_p[c] = single(pbuf.at[it + 1, core, rows[c]], partner)

    def squares(it, c):
        for k in range(c + 1):
            square = dot(pc[pieces[c]], pc[pieces[k]], NT)
            gbuf[it, core, c, :, 32 * k : 32 * k + 32] = fold2(square)
        swap_g[c] = single(gbuf.at[it, core, c], partner)

    swap_g = [None, None]
    moving = [product(0, c) for c in range(2)]
    for it in range(ITERS):
        if it > 0:
            swap_g[0].wait_recv()
            la, da = factor32(gbuf[it - 1, 0, 0, :, 0:32] + gbuf[it - 1, 1, 0, :, 0:32])
        moving[0] = second(it, 0, moving[0])
        if it > 0:
            swap_g[1].wait_recv()
            low = gbuf[it - 1, 0, 1, :, 0:64] + gbuf[it - 1, 1, 1, :, 0:64]
            lba, lb, db = lower(low, la)
            str_ref[it - 1 : it, :] = jnp.concatenate([da, db], axis=1)
        moving[1] = second(it, 1, moving[1])
        moving = [third(it, c, moving[c]) for c in range(2)]
        if it == ITERS - 1:
            break
        for c in range(2):
            done = raw = reduced(it, c, moving[c])
            if it > 0:
                done = exact(la, raw) if c == 0 else exact(lba, above) + exact(lb, raw)
            above = raw
            moving[c] = gather1(it, c, done)
        moving = [gather2(it, c, moving[c]) for c in range(2)]
        for c in range(2):
            projected(it, c, *moving[c])
        moving = [product(it + 1, c) for c in range(2)]
        for c in range(2):
            squares(it, c)

    it = ITERS - 1
    spot = x * 4 + z
    slabs, grams, wide = [], [], []
    for c in range(2):
        raw = reduced(it, c, moving[c])
        done = exact(la, raw) if c == 0 else exact(lba, above) + exact(lb, raw)
        above = raw
        wide.append(split3(done))
        gram = jnp.concatenate([fold2(dot(wide[c], wide[k], NT)) for k in range(c + 1)], axis=1)
        size = 8 * (c + 1)
        ga[c, spot, 0:size] = jnp.concatenate([gram[k : k + size] for k in range(0, 32, size)], axis=1)
        here = ga.at[c, spot, 0:size]
        grams.append(group(ga.at[c, 0:15, 0:size], [(here, here, device) for device in plane]))
        fin[z, rows[c]] = jnp.where(y < 2, done[:, 0:128], done[:, 128:256])
        here = fin.at[z, rows[c]]
        slabs.append(group(fin.at[0:3, rows[c]], [(here, here, zp[o]) for o in order]))
    for c in range(2):
        size = 8 * (c + 1)
        grams[c].wait_recv()
        total = [ga[c, k, 0:size] + ga[c, k + 1, 0:size] for k in range(0, 16, 2)]
        while len(total) > 1:
            total = [total[k] + total[k + 1] for k in range(0, len(total), 2)]
        gbuf[it, core, c, 0:size] = total[0]
        swap_g[c] = single(gbuf.at[it, core, c, 0:size], partner)
        if c == 0:
            swap_g[0].wait_recv()
            gram = gbuf[it, 0, 0, 0:8] + gbuf[it, 1, 0, 0:8]
            la, da = factor32(jnp.concatenate([gram[:, k : k + 32] for k in range(0, 128, 32)], axis=0))
    swap_g[1].wait_recv()
    gram = gbuf[it, 0, 1, 0:16] + gbuf[it, 1, 1, 0:16]
    lba, lb, db = lower(jnp.concatenate([gram[:, 0:64], gram[:, 64:128]], axis=0), la)
    str_ref[it : it + 1, :] = jnp.concatenate([da, db], axis=1)
    for copy in slabs:
        copy.wait_recv()
    slab = jnp.concatenate([fin[k] for k in range(4)], axis=1)
    scale = math.sqrt(8192)
    load_ref[0:32] = exact(la, slab[0:32]) * scale
    load_ref[32:64] = (exact(lba, slab[0:32]) + exact(lb, slab[32:64])) * scale
    for copy in pending:
        copy.wait_send()


def lower(gram, la):
    b = exact(gram[:, 0:32], la, NT)
    lb, db = factor32(gram[:, 32:64] - exact(b, b, NT))
    return -exact(exact(lb, b), la), lb, db


SEMS = 80


def local(days, returns, start_seed):
    seed = start_seed.T
    vm = pltpu.VMEM
    out = pl.pallas_call(
        functools.partial(kernel, days),
        out_shape=(
            jax.ShapeDtypeStruct((64, 512), F32),
            jax.ShapeDtypeStruct((3, 64), F32),
        ),
        in_specs=[pl.BlockSpec(memory_space=pltpu.HBM)] * 2,
        out_specs=[pl.BlockSpec(memory_space=pltpu.VMEM)] * 2,
        scratch_shapes=[
            vm((256, 4096), BF16),
            vm((128, 8192), BF16),
            vm((64, 8192), jnp.int32),
            vm((3, 2, 64, 256), F32),
            vm((192, 4096), BF16),
            vm((3, 2, 2, 4, 4, 32, 128), F32),
            vm((3, 2, 2, 3, 4, 32, 128), F32),
            vm((3, 2, 2, 4, 32, 128), F32),
            vm((3, 2, 2, 3, 32, 128), F32),
            vm((3, 2, 4, 2, 32, 128), F32),
            vm((2, 2, 2, 4, 4, 32, 128), F32),
            vm((3, 2, 2, 32, 128), F32),
            vm((4, 64, 128), F32),
            vm((2, 16, 16, 128), F32),
            pltpu.SemaphoreType.DMA((17,)),
            pltpu.SemaphoreType.DMA((SEMS,)),
            pltpu.SemaphoreType.DMA((SEMS,)),
        ],
        compiler_params=pltpu.CompilerParams(
            collective_id=0, has_side_effects=True, vmem_limit_bytes=67043328
        ),
        name="power",
    )(returns, seed)
    return out[0].T, out[1]


def solution(mesh):
    placed = (P(("gr", "gc"), None), P())
    return jax.shard_map(
        functools.partial(local, 16384), mesh=mesh, in_specs=placed,
        out_specs=(P("gr", None), P()), check_vma=False,
    )
```

```python
import functools
import math

import jax
import jax.numpy as jnp
from jax import lax
from jax.experimental import pallas as pl
from jax.experimental.pallas import tpu as pltpu
from jax.sharding import PartitionSpec as P

ITERS = 3
MESH = pl.DeviceIdType.MESH
F32 = jnp.float32
BF16 = jnp.bfloat16
NN = (((1,), (0,)), ((), ()))
NT = (((1,), (1,)), ((), ()))


def dot(a, b, dims=NN):
    return lax.dot_general(a, b, dims, preferred_element_type=F32)


def exact(a, b, dims=NN):
    return lax.dot_general(a, b, dims, precision=lax.Precision.HIGHEST, preferred_element_type=F32)


def split3(a):
    hi = a.astype(BF16)
    rest = a - hi.astype(F32)
    mid = rest.astype(BF16)
    low = (rest - mid.astype(F32)).astype(BF16)
    return jnp.concatenate([hi, mid, low], axis=0)


def fold(a):
    return a[0:32] + (a[32:64] + a[64:96])


def fold2(a):
    hh, hm, hl = a[0:32, 0:32], a[0:32, 32:64], a[0:32, 64:96]
    mh, mm, lh = a[32:64, 0:32], a[32:64, 32:64], a[64:96, 0:32]
    return hh + ((hm + mh) + (mm + (hl + lh)))


def factor32(gram):
    lane = lax.broadcasted_iota(jnp.int32, (8, 128), 1)
    sub = lax.broadcasted_iota(jnp.int32, (8, 128), 0)
    bc = lambda a: jnp.broadcast_to(a, (8, 128))
    zero = jnp.zeros((32, 32), F32)
    wide = jnp.concatenate([zero, zero, gram, zero], axis=1)
    rows = [jnp.where(lane == sub + 8 * g, 1.0, wide[8 * g : 8 * g + 8]) for g in range(4)]
    for j in range(0, 32, 4):
        g0, r = divmod(j, 8)
        cols = [[bc(rows[g][:, 64 + j + k : 65 + j + k]) for g in range(g0, 4)] for k in range(4)]
        p = [bc(rows[g0][r + k : r + k + 1, :]) for k in range(4)]
        a = [[bc(cols[k][0][r + i : r + i + 1, :]) for k in range(i + 1)] for i in range(4)]
        idet = 1.0 / (a[0][0] * a[1][1] - a[1][0] * a[1][0])
        s = (a[1][1] * p[0] - a[1][0] * p[1]) * idet
        t = (a[0][0] * p[1] - a[1][0] * p[0]) * idet
        s2 = (a[1][1] * a[2][0] - a[1][0] * a[2][1]) * idet
        t2 = (a[0][0] * a[2][1] - a[1][0] * a[2][0]) * idet
        s3 = (a[1][1] * a[3][0] - a[1][0] * a[3][1]) * idet
        t3 = (a[0][0] * a[3][1] - a[1][0] * a[3][0]) * idet
        a22 = a[2][2] - (a[2][0] * s2 + a[2][1] * t2)
        a32 = a[3][2] - (a[3][0] * s2 + a[3][1] * t2)
        a33 = a[3][3] - (a[3][0] * s3 + a[3][1] * t3)
        p2 = p[2] - (a[2][0] * s + a[2][1] * t)
        p3 = p[3] - (a[3][0] * s + a[3][1] * t)
        idet = 1.0 / (a22 * a33 - a32 * a32)
        u = (a33 * p2 - a32 * p3) * idet
        v = (a22 * p3 - a32 * p2) * idet
        s = s - (s2 * u + s3 * v)
        t = t - (t2 * u + t3 * v)
        for g in range(g0, 4):
            c = [cols[k][g - g0] for k in range(4)]
            new = rows[g] - ((c[0] * s + c[1] * t) + (c[2] * u + c[3] * v))
            if g == g0:
                p1 = p[1] - a[1][0] / a[0][0] * p[0]
                p3 = p3 - a32 / a22 * p2
                new = jnp.where(sub < r + 4, rows[g], new)
                new = jnp.where(sub == r + 1, p1, new)
                new = jnp.where(sub == r + 2, p2, new)
                new = jnp.where(sub == r + 3, p3, new)
            rows[g] = new
    inverse = []
    diag = jnp.zeros((8, 128), F32)
    for g in range(4):
        mask = lane == sub + (8 * g + 64)
        d = jnp.sum(jnp.where(mask, rows[g], 0.0), axis=1, keepdims=True)
        root = bc(jnp.sqrt(d))
        inverse.append(rows[g] / root)
        diag = diag + jnp.where(mask, root, 0.0)
    return jnp.concatenate(inverse, axis=0)[:, 0:32], jnp.sum(diag, axis=0, keepdims=True)[:, 64:96]


def kernel(
    days, r_ref, seed_ref, load_ref, str_ref,
    rb, rv, sv, pbuf, pc, abuf, r1, bbuf, r2, ybuf, ag, gbuf, fin, ga,
    local, send, recv,
):
    gr = lax.axis_index("gr")
    gc = lax.axis_index("gc")
    core = gr % 2
    x = gr // 4
    y = (gr // 2) % 2 * 2 + gc % 2
    z = gc // 2

    def dev(x, y, z, core):
        return ((x * 2 + y // 2) * 2 + core, z * 2 + y % 2)

    partner = dev(x, y, z, 1 - core)
    order = (1, 0, 2)
    xp = [dev((x + o) % 4, y, z, core) for o in (1, 2, 3)]
    yp = [dev(x, (y + o) % 4, z, core) for o in (1, 2, 3)]
    zp = [dev(x, y, (z + o) % 4, core) for o in (1, 2, 3)]
    plane = [dev((x + k // 4) % 4, y, (z + k % 4) % 4, core) for k in range(1, 16)]

    barrier = pltpu.get_barrier_semaphore()
    everyone = [partner] + xp + yp + zp
    for device in everyone:
        pl.semaphore_signal(barrier, inc=1, device_id=device, device_id_type=MESH)

    mine = pl.ds(pl.multiple_of(core * 128, 128), 128)
    loads = []
    for s in range(8):
        here = pl.ds(s * 1024, 1024)
        loads.append(
            (
                pltpu.make_async_copy(seed_ref.at[:, here], sv.at[:, here], local.at[s]),
                pltpu.make_async_copy(r_ref.at[:, here], rv.at[:, here], local.at[8 + s]),
            )
        )
        for copy in loads[s]:
            copy.start()
    spots = [(2 * q, 0, 512, q * 512) for q in range(4)]
    spots += [(2 * q + 1, j * 128, 128, 2048 + j * 512 + q * 128) for q in range(4) for j in range(4)]

    def columns(slab, offset, width, side):
        return r_ref.at[:, pl.ds(pl.multiple_of((slab * 2 + side) * 512 + offset, 128), width)]

    for slab, offset, width, spot in spots:
        here = rb.at[mine, pl.ds(spot, width)]
        pltpu.make_async_copy(columns(slab, offset, width, core), here, local.at[16]).start()
    halves = pltpu.make_async_copy(r_ref.at[:, 0:4096], rb.at[mine], local.at[16])

    pl.semaphore_wait(barrier, len(everyone))

    count = [0]
    pending = []

    def group(region, parts):
        k = count[0]
        count[0] += 1
        for src, dst, device in parts:
            pltpu.make_async_remote_copy(
                src_ref=src, dst_ref=dst, send_sem=send.at[k], recv_sem=recv.at[k],
                device_id=device, device_id_type=MESH,
            ).start()
        whole = pltpu.make_async_remote_copy(
            src_ref=region, dst_ref=region, send_sem=send.at[k], recv_sem=recv.at[k],
            device_id=partner, device_id_type=MESH,
        )
        pending.append(whole)
        return whole

    def finish():
        while pending:
            pending.pop().wait_send()

    def single(ref, device):
        return group(ref, [(ref, ref, device)])

    swaps = group(
        rb.at[0:128],
        [
            (columns(slab, offset, width, 1 - core), rb.at[mine, pl.ds(spot, width)], partner)
            for slab, offset, width, spot in spots
        ],
    )

    rows = [slice(32 * c, 32 * c + 32) for c in range(2)]
    pieces = [slice(96 * c, 96 * c + 96) for c in range(2)]
    def either(a, b):
        return core * a + (1 - core) * b

    def mix(a, b):
        return either(a[0], b[0]), [tuple(either(m, n) for m, n in zip(i, j)) for i, j in zip(a[1], b[1])]

    ax, ay, az = (x, xp), (y, yp), (z, zp)
    streams = (
        (((ax, az, ay), (az, ay, ax)), ((ay, ax, az), (mix(az, ax), mix(ax, az), ay))),
        (((ax, az, ay), (az, ax, ay)), ((ax, az, ay), (az, ax, ay))),
    )
    place = [[[[d[0] for d in h] for h in c] for c in r] for r in streams]
    peers = [[[[d[1] for d in h] for h in c] for c in r] for r in streams]
    swap_p = [None, None]

    first = None
    for s in range(8):
        here = slice(s * 1024, (s + 1) * 1024)
        for copy in loads[s]:
            copy.wait()
        part = sv[:, here].astype(F32)
        hi = part.astype(BF16)
        part = jnp.concatenate([hi, (part - hi.astype(F32)).astype(BF16)], axis=0)
        part = dot(part, rv[:, here], NT)
        first = part if first is None else first + part
    first = (first[0:64] + first[64:128]) / 1000.0
    pbuf[0, core, :, 0:128] = first
    swap_p[0] = single(pbuf.at[0, core, :, 0:128], partner)
    halves.wait()
    swap_p[0].wait_recv()
    first = jnp.concatenate([pbuf[0, 0, :, 0:128], pbuf[0, 1, :, 0:128]], axis=1)
    swaps.wait_recv()

    def part(h, p):
        return pl.ds(pl.multiple_of(h * 2048 + p * 512, 512), 512)

    def product(it, c):
        if it > 0:
            swap_p[c].wait_recv()
            p3 = split3((pbuf[it, 0, rows[c]] + pbuf[it, 1, rows[c]]) * (1.0 / days))
        else:
            p3 = split3(first[rows[c]] * (1.0 / days))
        moving = []

        def go(o):
            parts = []
            for h in range(2):
                to = (place[it > 0][c][h][0] + o + 1) % 4
                parts.append((abuf.at[it, c, h, to], r1.at[it, c, h, o], peers[it > 0][c][h][0][o]))
            return parts

        for o in order + (3,):
            for h in range(2):
                to = (place[it > 0][c][h][0] + o + 1) % 4
                out = fold(dot(p3, rb[:, part(h, to)]))
                for j in range(4):
                    abuf[it, c, h, to, j] = out[:, j * 128 : (j + 1) * 128]
            if o == 0:
                moving.append(group(r1.at[it, c, :, 0:2], go(1) + go(0)))
            elif o == 2:
                moving.append(group(r1.at[it, c, 0, 0:2], go(2)))
        return moving

    def second(it, c, moving):
        for copy in moving:
            copy.wait_recv()
        parts = []
        for h in range(2):
            bbuf[it, c, h] = (abuf[it, c, h, place[it > 0][c][h][0]] + r1[it, c, h, 0]) + (r1[it, c, h, 1] + r1[it, c, h, 2])
            for o in order:
                to = (place[it > 0][c][h][1] + o + 1) % 4
                parts.append((bbuf.at[it, c, h, to], r2.at[it, c, h, o], peers[it > 0][c][h][1][o]))
        return group(r2.at[it, c], parts)

    def third(it, c, moving):
        moving.wait_recv()
        for h in range(2):
            ybuf[it, c, place[it > 0][c][h][2], h] = (bbuf[it, c, h, place[it > 0][c][h][1]] + r2[it, c, h, 0]) + (r2[it, c, h, 1] + r2[it, c, h, 2])
        parts = []
        for h in range(2):
            here = ybuf.at[it, c, place[it > 0][c][h][2], h]
            parts += [(here, here, peers[it > 0][c][h][2][o]) for o in order]
        return group(ybuf.at[it, c, 0:3], parts)

    def reduced(it, c, moving):
        moving.wait_recv()
        return jnp.concatenate(
            [(ybuf[it, c, 0, h] + ybuf[it, c, 1, h]) + (ybuf[it, c, 2, h] + ybuf[it, c, 3, h]) for h in range(2)],
            axis=1,
        )

    def gather1(it, c, done):
        parts = []
        for h in range(2):
            ag[it, c, h, place[it > 0][c][h][0], place[it > 0][c][h][1]] = done[:, 128 * h : 128 * h + 128]
        for h in range(2):
            block = ag.at[it, c, h, place[it > 0][c][h][0], place[it > 0][c][h][1]]
            parts += [(block, block, peers[it > 0][c][h][1][o]) for o in order]
        near = group(r2.at[it, c], parts)
        parts = []
        for h in range(2):
            block = ag.at[it, c, h, place[it > 0][c][h][0], place[it > 0][c][h][1]]
            parts += [(block, block, peers[it > 0][c][h][0][o]) for o in order]
        return near, group(r2.at[it, c], parts)

    def gather2(it, c, moving):
        moving[0].wait_recv()
        sent = [moving[1]]
        for o in order:
            parts = []
            for h in range(2):
                for k in (1, 2, 3):
                    block = ag.at[it, c, h, place[it > 0][c][h][0], (place[it > 0][c][h][1] + k) % 4]
                    parts.append((block, block, peers[it > 0][c][h][0][o]))
            sent.append(group(r2.at[it, c], parts))
        return sent, project(it, c, 3)

    def project(it, c, o):
        total = None
        for h in range(2):
            p = (place[it > 0][c][h][0] + 3 - o) % 4
            piece = split3(jnp.concatenate([ag[it, c, h, p, j] for j in range(4)], axis=1))
            pc[pieces[c], part(h, p)] = piece
            term = dot(piece, rb[:, part(h, p)], NT)
            total = term if total is None else total + term
        return total

    def projected(it, c, sent, total):
        sent[0].wait_recv()
        for o, copy in zip(order, sent[1:]):
            copy.wait_recv()
            total = total + project(it, c, o)
        pbuf[it + 1, core, rows[c]] = fold(total)
        swap_p[c] = single(pbuf.at[it + 1, core, rows[c]], partner)

    def squares(it, c):
        for k in range(c + 1):
            square = dot(pc[pieces[c]], pc[pieces[k]], NT)
            gbuf[it, core, c, :, 32 * k : 32 * k + 32] = fold2(square)
        swap_g[c] = single(gbuf.at[it, core, c], partner)

    swap_g = [None, None]
    moving = [product(0, 0)]
    moving.append(product(0, 1))
    for it in range(ITERS):
        if it > 0:
            swap_g[0].wait_recv()
            la, da = factor32(gbuf[it - 1, 0, 0, :, 0:32] + gbuf[it - 1, 1, 0, :, 0:32])
        moving[0] = second(it, 0, moving[0])
        moving[1] = second(it, 1, moving[1])
        if it > 0:
            swap_g[1].wait_recv()
            low = gbuf[it - 1, 0, 1, :, 0:64] + gbuf[it - 1, 1, 1, :, 0:64]
            lba, lb, db = lower(low, la)
            str_ref[it - 1 : it, :] = jnp.concatenate([da, db], axis=1)
        moving = [third(it, c, moving[c]) for c in range(2)]
        if it == ITERS - 1:
            break
        for c in range(2):
            done = raw = reduced(it, c, moving[c])
            if it > 0:
                done = exact(la, raw) if c == 0 else exact(lba, above) + exact(lb, raw)
            above = raw
            moving[c] = gather1(it, c, done)
        moving = [gather2(it, c, moving[c]) for c in range(2)]
        projected(it, 0, *moving[0])
        late = moving[1]
        moving = [product(it + 1, 0)]
        projected(it, 1, *late)
        moving.append(product(it + 1, 1))
        squares(it, 0)
        squares(it, 1)

    it = ITERS - 1
    spot = x * 4 + z
    slabs, grams, wide = [], [], []
    for c in range(2):
        raw = reduced(it, c, moving[c])
        done = exact(la, raw) if c == 0 else exact(lba, above) + exact(lb, raw)
        above = raw
        wide.append(split3(done))
        gram = jnp.concatenate([fold2(dot(wide[c], wide[k], NT)) for k in range(c + 1)], axis=1)
        size = 8 * (c + 1)
        ga[c, spot, 0:size] = jnp.concatenate([gram[k : k + size] for k in range(0, 32, size)], axis=1)
        here = ga.at[c, spot, 0:size]
        grams.append(group(ga.at[c, 0:15, 0:size], [(here, here, device) for device in plane]))
        fin[z, rows[c]] = jnp.where(y < 2, done[:, 0:128], done[:, 128:256])
        here = fin.at[z, rows[c]]
        slabs.append(group(fin.at[0:3, rows[c]], [(here, here, zp[o]) for o in order]))
    for c in range(2):
        size = 8 * (c + 1)
        grams[c].wait_recv()
        total = [ga[c, k, 0:size] + ga[c, k + 1, 0:size] for k in range(0, 16, 2)]
        while len(total) > 1:
            total = [total[k] + total[k + 1] for k in range(0, len(total), 2)]
        gbuf[it, core, c, 0:size] = total[0]
        swap_g[c] = single(gbuf.at[it, core, c, 0:size], partner)
        if c == 0:
            swap_g[0].wait_recv()
            gram = gbuf[it, 0, 0, 0:8] + gbuf[it, 1, 0, 0:8]
            la, da = factor32(jnp.concatenate([gram[:, k : k + 32] for k in range(0, 128, 32)], axis=0))
            for copy in slabs:
                copy.wait_recv()
            slab = jnp.concatenate([fin[k] for k in range(4)], axis=1)
            upper = exact(la, slab[0:32])
            scale = math.sqrt(8192)
            load_ref[0:32] = upper * scale
            finish()
    swap_g[1].wait_recv()
    gram = gbuf[it, 0, 1, 0:16] + gbuf[it, 1, 1, 0:16]
    gram = jnp.concatenate([gram[:, 0:64], gram[:, 64:128]], axis=0)
    cross = exact(gram[:, 0:32], la, NT)
    rest = slab[32:64] - exact(cross, upper)
    lb, db = factor32(gram[:, 32:64] - exact(cross, cross, NT))
    load_ref[32:64] = exact(lb, rest) * scale
    str_ref[it : it + 1, :] = jnp.concatenate([da, db], axis=1)
    finish()


def lower(gram, la):
    b = exact(gram[:, 0:32], la, NT)
    lb, db = factor32(gram[:, 32:64] - exact(b, b, NT))
    return -exact(exact(lb, b), la), lb, db


SEMS = 60


def local(days, returns, start_seed):
    seed = start_seed.T
    vm = pltpu.VMEM
    out = pl.pallas_call(
        functools.partial(kernel, days),
        out_shape=(
            jax.ShapeDtypeStruct((64, 512), F32),
            jax.ShapeDtypeStruct((3, 64), F32),
        ),
        in_specs=[pl.BlockSpec(memory_space=pltpu.HBM)] * 2,
        out_specs=[pl.BlockSpec(memory_space=pltpu.VMEM)] * 2,
        scratch_shapes=[
            vm((256, 4096), BF16),
            vm((128, 8192), BF16),
            vm((64, 8192), jnp.int32),
            vm((3, 2, 64, 256), F32),
            vm((192, 4096), BF16),
            vm((3, 2, 2, 4, 4, 32, 128), F32),
            vm((3, 2, 2, 3, 4, 32, 128), F32),
            vm((3, 2, 2, 4, 32, 128), F32),
            vm((3, 2, 2, 3, 32, 128), F32),
            vm((3, 2, 4, 2, 32, 128), F32),
            vm((2, 2, 2, 4, 4, 32, 128), F32),
            vm((3, 2, 2, 32, 128), F32),
            vm((4, 64, 128), F32),
            vm((2, 16, 16, 128), F32),
            pltpu.SemaphoreType.DMA((17,)),
            pltpu.SemaphoreType.DMA((SEMS,)),
            pltpu.SemaphoreType.DMA((SEMS,)),
        ],
        compiler_params=pltpu.CompilerParams(
            collective_id=0, has_side_effects=True, vmem_limit_bytes=67043328
        ),
        name="power",
    )(returns, seed)
    return out[0].T, out[1]


def solution(mesh):
    placed = (P(("gr", "gc"), None), P())
    return jax.shard_map(
        functools.partial(local, 16384), mesh=mesh, in_specs=placed,
        out_specs=(P("gr", None), P()), check_vma=False,
    )
```
